32 devices in a mesh: grp: 2 (over y), cell: 16 (over z, x, core).
Axes of the slice: x: 2, y: 2, z: 4, core: 2. Of those that a mesh axis runs over, the one named last changes fastest.
Arguments:
- momenta: int32 [3, 65536], replicated, may hold values from 1 to 32
- positions: float32 [3, 4096], P(None, ('grp', 'cell')), parts along dimension 1, may hold values from 0 to 1
- weights: bfloat16 [8, 4096], P(None, ('grp', 'cell')), parts along dimension 1, may hold values from 0.099609375 to 2
- triplets: int32 [3, 16384], P(None, ('grp', 'cell')), parts along dimension 1, may hold values from 0 to 65535, as said below
- cotangent: float32 [8, 16384], P(None, ('grp', 'cell')), parts along dimension 1, may hold values from -6 to 6
Outputs:
- correlation: float32 [8, 16384], P(None, ('grp', 'cell')), parts along dimension 1
- weight_grad: float32 [8, 4096], P(None, ('grp', 'cell')), parts along dimension 1
The draws below stay inside these ranges and needn't reach their ends.
There are 2 independent parts, one for each index of `grp`. The reference program is written for one: setup_inputs(seed, part) draws one part's arguments, and reference() takes and returns one part's arrays. A program takes and returns all parts, laid end to end along the dimension named above; an argument that names none is the same for every part. Nothing has to cross between parts.
Inputs may be any that keep to these rules, and one draw needn't show every extreme that they name: Among the 1536 momentum indices of one device's triplets, each block of 4096 momenta (4096 * r to 4096 * r + 4095) is named either 96 - 1 or 96 times.
All inputs are finite; a program needn't handle non-finite values.
Results may differ from the reference program's by a relative error of at most 0.0051.
Values may be sent and summed in bfloat16 or wider, within the bound.
No kernel may reach another device: no remote copies, remote signals or barrier semaphores. Data moves between devices by JAX's collectives and lax.ppermute only.
A program may use at most 256 MiB of HBM per device.

```python
import math
import jax
import jax.numpy as jnp
from jax import lax

K = 8
NQ = 65536
TRIP_DEV = 512
CELLS = 2048
TRIPLETS = 8192
OWNED = 4096
N_CELL = 16


def draw_triplets(key, part):

    def one_device(device_key):
        key_one, key_two = jax.random.split(device_key)
        shuffled = jax.random.permutation(key_one, 3 * TRIP_DEV)
        owner = shuffled % N_CELL
        offset = jax.random.randint(key_two, (3 * TRIP_DEV,), 0, OWNED)
        return (owner * OWNED + offset).astype(jnp.int32).reshape(3, TRIP_DEV)
    device_keys = jax.random.split(jax.random.fold_in(key, 7), N_CELL)
    blocks = jax.vmap(one_device)(device_keys)
    return blocks.transpose(1, 0, 2).reshape(3, TRIPLETS)


def touch_ends(array, rng, least, high):
    shape = array.shape
    spot = [jax.random.randint(jax.random.fold_in(rng, axis), (), 0, shape[axis]) for axis in range(len(shape))]
    array = array.at[tuple(spot)].set(least)
    longest = shape.index(max(shape))
    spot[longest] = (spot[longest] + 1) % shape[longest]
    return array.at[tuple(spot)].set(high)


def block_scale(key, extent, cuts, smallest, top_value):
    loudness, own = 1.0, jax.random.fold_in(key, 6)
    for axis_at, blocks in cuts:
        draws = jnp.exp(jax.random.uniform(jax.random.fold_in(own, axis_at), (blocks,), jnp.float32, smallest / len(cuts), top_value / len(cuts)))
        loudness = loudness * jnp.repeat(draws, extent[axis_at] // blocks).reshape([-1 if axis == axis_at else 1 for axis in range(len(extent))])
    return loudness


def normal_values(own_key, extent, width, limit, cuts=(), dtype=jnp.bfloat16):
    gain = block_scale(own_key, extent, cuts, -0.22, 0.18) if cuts else 1.0
    array = jax.random.normal(own_key, extent, jnp.float32) * width * gain
    return jnp.minimum(jnp.maximum(array, -limit), limit).astype(dtype)


def setup_inputs(seed: int = 0, part: int = 0) -> dict:
    streams_of = jax.random.split(jax.random.key(seed), 6)
    own_keys = jax.random.split(jax.random.fold_in(streams_of[5], part), 6)
    return {
        "momenta": touch_ends(jax.random.randint(streams_of[0], (3, NQ), 1, 33), jax.random.fold_in(streams_of[0], 1), 1, 32).astype(jnp.int32),
        "positions": jnp.clip(1.0 * jax.random.uniform(own_keys[1], (3, CELLS), jnp.float32) ** block_scale(own_keys[1], (3, CELLS), ((1, 16),), -0.2, 0.2), 0.0, 1.0),
        "weights": jnp.clip(jnp.exp(math.log(2.0) - 2.9996462 * jax.random.uniform(own_keys[2], (K, CELLS), jnp.float32) ** block_scale(own_keys[2], (K, CELLS), ((1, 16),), -0.2, 0.2)), 0.099609375, 2.0).astype(jnp.bfloat16),
        "triplets": draw_triplets(jax.random.fold_in(jax.random.fold_in(streams_of[5], part), 71), part),
        "cotangent": normal_values(own_keys[4], (K, TRIPLETS), 1.0, 6.0, ((1, 16),), jnp.float32),
    }


TWO_PI = 2.0 * math.pi

def tables(moment_block, position_block):
    numbers = moment_block.astype(jnp.float32)
    phase = numbers[0][:, None] * position_block[0][None, :]
    phase = phase + numbers[1][:, None] * position_block[1][None, :]
    phase = phase + numbers[2][:, None] * position_block[2][None, :]
    phase = TWO_PI * phase
    return (jnp.cos(phase).astype(jnp.bfloat16), jnp.sin(phase).astype(jnp.bfloat16))

def contract(left, right):
    return lax.dot_general(left, right, (((1,), (1,)), ((), ())), preferred_element_type=jnp.float32)

def couple(cotangent, real_one, imag_one, real_two, imag_two):
    real_part = cotangent * (real_one * real_two - imag_one * imag_two)
    imag_part = -cotangent * (imag_one * real_two + real_one * imag_two)
    return jnp.concatenate([real_part, imag_part], 0)

def triplet_terms(amplitude, triplets, cotangent, bin_count):
    real_rows = amplitude[:bin_count]
    imag_rows = amplitude[bin_count:]
    real_a = real_rows[:, triplets[0]]
    real_b = real_rows[:, triplets[1]]
    real_c = real_rows[:, triplets[2]]
    imag_a = imag_rows[:, triplets[0]]
    imag_b = imag_rows[:, triplets[1]]
    imag_c = imag_rows[:, triplets[2]]
    correlation = real_a * real_b * real_c - real_a * imag_b * imag_c - imag_a * real_b * imag_c - imag_a * imag_b * real_c
    adjoint = jnp.zeros(amplitude.shape, jnp.float32)
    adjoint = adjoint.at[:, triplets[0]].add(couple(cotangent, real_b, imag_b, real_c, imag_c))
    adjoint = adjoint.at[:, triplets[1]].add(couple(cotangent, real_a, imag_a, real_c, imag_c))
    adjoint = adjoint.at[:, triplets[2]].add(couple(cotangent, real_a, imag_a, real_b, imag_b))
    return (correlation, adjoint)

def reference(momenta, positions, weights, triplets, cotangent):
    bin_count = weights.shape[0]
    cell_count = positions.shape[1]
    moment_count = momenta.shape[1]
    cell_step = min(cell_count, 256)
    block_count = cell_count // cell_step
    pos_blocks = positions.reshape(3, block_count, cell_step).transpose(1, 0, 2)
    weight_blocks = weights.reshape(bin_count, block_count, cell_step).transpose(1, 0, 2)

    def forward(summed, block_item):
        pos_block, weight_block = block_item
        cosine, sine = tables(momenta, pos_block)
        term = jnp.concatenate([contract(weight_block, cosine), contract(weight_block, sine)], 0)
        return (summed + term, None)
    summed, _ = lax.scan(forward, jnp.zeros((2 * bin_count, moment_count), jnp.float32), (pos_blocks, weight_blocks))
    norm_factor = 1.0 / math.sqrt(cell_count)
    amplitude = summed * norm_factor
    correlation, adjoint = triplet_terms(amplitude, triplets, cotangent, bin_count)
    scaled_adjoint = (adjoint * norm_factor).astype(jnp.bfloat16)

    def backward(pos_block):
        cosine, sine = tables(momenta, pos_block)
        return jnp.dot(scaled_adjoint[:bin_count], cosine, preferred_element_type=jnp.float32) + jnp.dot(scaled_adjoint[bin_count:], sine, preferred_element_type=jnp.float32)
    grads = lax.map(backward, pos_blocks)
    weight_grad = grads.transpose(1, 0, 2).reshape(bin_count, cell_count)
    return (correlation, weight_grad)
```

```python
import functools
import math

import jax
import jax.numpy as jnp
import numpy as np
from jax import lax
from jax.experimental import pallas as pl
from jax.experimental.pallas import tpu as pltpu
from jax.sharding import PartitionSpec as P

LANES = 128
ROWS = 16
DEPTH = 32
CELL_STEP = 256
SLOT_STEP = 256
KEEP_BYTES = 24 << 20


def fit(values, terms):
    nodes = 0.125 + 0.125 * np.cos(np.pi * (np.arange(64) + 0.5) / 64)
    series = np.polynomial.chebyshev.Chebyshev.fit(nodes, values(np.sqrt(nodes)), terms - 1, domain=[0.0, 0.25])
    return [float(c) for c in series.convert(kind=np.polynomial.Polynomial).coef]


SINE = fit(lambda f: math.sqrt(2.0) * np.sin(np.pi * f) / f, 4)
COSINE = fit(lambda f: math.sqrt(2.0) * np.cos(np.pi * f), 5)


def series_of(u, coefficients):
    total = coefficients[-1] * u + coefficients[-2]
    for c in coefficients[-3::-1]:
        total = total * u + c
    return total


def cos_sin(turns):
    f = turns - jnp.round(turns)
    u = f * f
    s = f * series_of(u, SINE)
    c = series_of(u, COSINE)
    return 1.0 - s * s, s * c


def lookup_kernel(tri_ref, table_ref, out_ref):
    rows = table_ref.shape[0]
    width = tri_ref.shape[1]
    lane_iota = lax.broadcasted_iota(jnp.int32, (LANES, width), 0)
    row_iota = lax.broadcasted_iota(jnp.int32, (rows, width), 0)
    parts = [table_ref[:, d, :].astype(jnp.float32).astype(jnp.bfloat16) for d in range(3)]
    for place in range(3):
        index = tri_ref[place : place + 1, :]
        pick = jnp.where(lane_iota == (index & (LANES - 1)), 1.0, 0.0).astype(jnp.bfloat16)
        hit = row_iota == (index >> 7)
        found = []
        for d in range(3):
            line = jnp.dot(parts[d], pick, preferred_element_type=jnp.float32)
            found.append(jnp.sum(jnp.where(hit, line, 0.0), axis=0, keepdims=True))
        found.append(jnp.zeros((5, width), jnp.float32))
        eight = jnp.concatenate(found, axis=0)
        wide = jnp.concatenate([eight, eight, eight, jnp.zeros((LANES - 24, width), jnp.float32)], axis=0)
        out_ref[place * width : (place + 1) * width, :] = wide.T.astype(jnp.bfloat16)


def main_kernel(keep, norm, data_ref, slot_ref, cot_ref, corr_ref, grad_ref, x_ref, w_ref, turn_ref, cos_ref, sin_ref):
    blocks = data_ref.shape[0]
    slots = slot_ref.shape[0]
    width = cot_ref.shape[1]
    cells = blocks * LANES
    cell_steps = cells // CELL_STEP
    slot_steps = slots // SLOT_STEP
    per_step = CELL_STEP // LANES

    def prepare(j, carry):
        at = pl.ds(pl.multiple_of(j * LANES, LANES), LANES)
        place = data_ref[j, 0:8, :]
        place = place - jnp.round(place)
        high = place.astype(jnp.bfloat16).astype(jnp.float32)
        rest = place - high
        middle = rest.astype(jnp.bfloat16).astype(jnp.float32)
        low = rest - middle
        x_ref[:, at] = jnp.concatenate([high, middle, low, jnp.zeros_like(low)], axis=0).astype(jnp.bfloat16)
        w_ref[:, at] = data_ref[j, 8:16, :].astype(jnp.bfloat16)
        return carry

    lax.fori_loop(0, blocks, prepare, 0)

    def fill(step, slot_at):
        at = pl.ds(pl.multiple_of(step * CELL_STEP, CELL_STEP), CELL_STEP)
        to = pl.ds(pl.multiple_of(slot_at * CELL_STEP, CELL_STEP), CELL_STEP)
        x = x_ref[:, at]

        def some(b, carry):
            base = pl.multiple_of(b * SLOT_STEP, SLOT_STEP)
            turn_ref[...] = jnp.dot(slot_ref[pl.ds(base, SLOT_STEP), 0:DEPTH], x, preferred_element_type=jnp.float32)
            for r in range(0, SLOT_STEP, 16):
                c, s = cos_sin(turn_ref[r : r + 16, :])
                here = pl.ds(pl.multiple_of(base + r, 16), 16)
                cos_ref[here, to] = c.astype(jnp.bfloat16)
                sin_ref[here, to] = s.astype(jnp.bfloat16)
            return carry

        lax.fori_loop(0, slot_steps, some, 0)
        return at, to

    def over_slots(left, right):
        return lax.dot_general(left, right, (((1,), (1,)), ((), ())), preferred_element_type=jnp.float32)

    def forward(step, sums):
        at, to = fill(step, step if keep else 0)
        w = w_ref[:, at]
        return sums[0] + over_slots(w, cos_ref[:, to]), sums[1] + over_slots(w, sin_ref[:, to])

    zero = jnp.zeros((8, slots), jnp.float32)
    real, imag = lax.fori_loop(0, cell_steps, forward, (zero, zero))
    real, imag = real * norm, imag * norm
    ar, br, cr = (real[:, p * width : (p + 1) * width] for p in range(3))
    ai, bi, ci = (imag[:, p * width : (p + 1) * width] for p in range(3))
    cot = cot_ref[...]
    bcr, bci = br * cr - bi * ci, br * ci + bi * cr
    corr_ref[...] = ar * bcr - ai * bci
    acr, aci = ar * cr - ai * ci, ar * ci + ai * cr
    abr, abi = ar * br - ai * bi, ar * bi + ai * br
    scaled = cot * norm
    left_real = jnp.concatenate([scaled * bcr, scaled * acr, scaled * abr], axis=1).astype(jnp.bfloat16)
    left_imag = jnp.concatenate([-scaled * bci, -scaled * aci, -scaled * abi], axis=1).astype(jnp.bfloat16)

    def backward(step, carry):
        if keep:
            to = pl.ds(pl.multiple_of(step * CELL_STEP, CELL_STEP), CELL_STEP)
        else:
            _, to = fill(step, 0)
        out = jnp.dot(left_real, cos_ref[:, to], preferred_element_type=jnp.float32) + jnp.dot(
            left_imag, sin_ref[:, to], preferred_element_type=jnp.float32
        )
        for i in range(per_step):
            grad_ref[step * per_step + i] = out[:, i * LANES : (i + 1) * LANES]
        return carry

    lax.fori_loop(0, cell_steps, backward, 0)


def lookup(triplets, momenta):
    count = momenta.shape[1]
    table = momenta.reshape(3, count // LANES, LANES).transpose(1, 0, 2)
    slots = 3 * triplets.shape[1]
    return pl.pallas_call(
        lookup_kernel, out_shape=jax.ShapeDtypeStruct((slots, LANES), jnp.bfloat16), name="lookup"
    )(triplets, table)


def triplet_stage(data, slot_rows, cotangent):
    blocks = data.shape[0]
    slots = slot_rows.shape[0]
    cells = blocks * LANES
    keep = 4 * slots * cells <= KEEP_BYTES
    kept = cells if keep else CELL_STEP
    return pl.pallas_call(
        functools.partial(main_kernel, keep, 1.0 / math.sqrt(cells)),
        out_shape=(
            jax.ShapeDtypeStruct(cotangent.shape, jnp.float32),
            jax.ShapeDtypeStruct((blocks, 8, LANES), jnp.float32),
        ),
        scratch_shapes=[
            pltpu.VMEM((DEPTH, cells), jnp.bfloat16),
            pltpu.VMEM((8, cells), jnp.bfloat16),
            pltpu.VMEM((SLOT_STEP, CELL_STEP), jnp.float32),
            pltpu.VMEM((slots, kept), jnp.bfloat16),
            pltpu.VMEM((slots, kept), jnp.bfloat16),
        ],
        name="triplet_stage",
    )(data, slot_rows, cotangent)


def strides(devices):
    return [1 << i for i in range(devices.bit_length() - 1)]


def gather_cells(block, devices):
    held = block[None]
    for stride in strides(devices):
        pairs = [(i, i ^ stride) for i in range(devices)]
        held = jnp.concatenate([held, lax.ppermute(held, "cell", pairs)], axis=0)
    return held


def reduce_cells(blocks, devices):
    for stride in reversed(strides(devices)):
        pairs = [(i, i ^ stride) for i in range(devices)]
        blocks = blocks[:stride] + lax.ppermute(blocks[stride:], "cell", pairs)
    return blocks[0]


def on_device(momenta, positions, weights, triplets, cotangent):
    devices = lax.axis_size("cell")
    block = jnp.concatenate(
        [positions, jnp.zeros((5, positions.shape[1]), jnp.float32), weights.astype(jnp.float32)], axis=0
    )
    data = gather_cells(block, devices)
    slot_rows = lookup(triplets, momenta)
    correlation, partial = triplet_stage(data, slot_rows, cotangent)
    return correlation, reduce_cells(partial, devices)


def solution(mesh):
    split = P(None, ("grp", "cell"))
    return jax.shard_map(
        on_device,
        mesh=mesh,
        in_specs=(P(), split, split, split, split),
        out_specs=(split, split),
        check_vma=False,
    )
```

```python
import functools
import math

import jax
import jax.numpy as jnp
import numpy as np
from jax import lax
from jax.experimental import pallas as pl
from jax.experimental.pallas import tpu as pltpu
from jax.sharding import PartitionSpec as P

LANES = 128
WIDE = 256
ROWS = 16
DEPTH = 32
CELL_STEP = 256
SLOT_STEP = 512
KEEP_BYTES = 24 << 20


def fit(values, terms):
    nodes = 0.125 + 0.125 * np.cos(np.pi * (np.arange(64) + 0.5) / 64)
    series = np.polynomial.chebyshev.Chebyshev.fit(nodes, values(np.sqrt(nodes)), terms - 1, domain=[0.0, 0.25])
    all_of = series.convert(kind=np.polynomial.Polynomial).coef
    return [float(c / all_of[-1]) for c in all_of[:-1]], float(all_of[-1])


SINE, SINE_TOP = fit(lambda f: np.sin(0.5 * np.pi * f) / f, 3)
COSINE, COSINE_TOP = fit(lambda f: np.cos(0.5 * np.pi * f), 4)
HALF_COSINE = 2.0 * SINE_TOP * SINE_TOP
COS_UNIT = 2.0 ** round(math.log2(8.0 * (SINE_TOP * COSINE_TOP) ** 2))
HALF_SINE = math.sqrt(0.5 * COS_UNIT)
RATIO = 2.0 * SINE_TOP * COSINE_TOP / HALF_SINE
SIN_UNIT = 2.0 * HALF_SINE * HALF_COSINE


def series_of(u, top, coefficients):
    total = (u if top == 1.0 else top * u) + coefficients[-1]
    for c in coefficients[-2::-1]:
        total = total * u + c
    return total


def cos_sin(turns):
    f = turns - jnp.round(turns)
    u = f * f
    s = f * series_of(u, 1.0, SINE)
    c = series_of(u, RATIO, [RATIO * v for v in COSINE])
    half = s * c
    return 1.0 / COS_UNIT - half * half, half * (1.0 / HALF_COSINE - s * s)


def lookup_kernel(tri_ref, table_ref, out_ref):
    rows = table_ref.shape[0]
    width = tri_ref.shape[1]
    lane_iota = lax.broadcasted_iota(jnp.int32, (WIDE, width), 0)
    row_iota = lax.broadcasted_iota(jnp.int32, (rows, width), 0)
    table = table_ref[...]
    bytes_of = jnp.concatenate([table & 255, table - (table & 255)], axis=1)
    left = bytes_of.astype(jnp.float32).astype(jnp.bfloat16)
    for place in range(3):
        index = tri_ref[place : place + 1, :]
        pick = jnp.where(lane_iota == (index & (WIDE - 1)), 1.0, 0.0).astype(jnp.bfloat16)
        line = jnp.dot(left, jnp.concatenate([pick, pick], axis=0), preferred_element_type=jnp.float32)
        code = jnp.sum(jnp.where(row_iota == (index >> (WIDE.bit_length() - 1)), line, 0.0), axis=0, keepdims=True)
        third = jnp.floor(code * (1.0 / 1024.0))
        rest = code - 1024.0 * third
        second = jnp.floor(rest * (1.0 / 32.0))
        first = rest - 32.0 * second
        eight = jnp.concatenate([first + 1.0, second + 1.0, third + 1.0, jnp.zeros((5, width), jnp.float32)], axis=0)
        wide = jnp.concatenate([eight, eight, eight, jnp.zeros((LANES - 24, width), jnp.float32)], axis=0)
        out_ref[place * width : (place + 1) * width, :] = wide.T.astype(jnp.bfloat16)


def main_kernel(keep, norm, data_ref, slot_ref, cot_ref, corr_ref, grad_ref, x_ref, w_ref, sum_ref, cos_ref, sin_ref):
    blocks = data_ref.shape[0]
    slots = slot_ref.shape[0]
    width = cot_ref.shape[1]
    cells = blocks * LANES
    cell_steps = cells // CELL_STEP
    slot_steps = slots // SLOT_STEP
    per_step = CELL_STEP // LANES

    def prepare(j, carry):
        at = pl.ds(pl.multiple_of(j * LANES, LANES), LANES)
        place = data_ref[j, 0:8, :]
        place = place - jnp.round(place)
        high = place.astype(jnp.bfloat16).astype(jnp.float32)
        rest = place - high
        middle = rest.astype(jnp.bfloat16).astype(jnp.float32)
        low = rest - middle
        none = jnp.zeros_like(low)
        x_ref[:, at] = jnp.concatenate([high, middle, low, none], axis=0).astype(jnp.bfloat16)
        w_ref[:, at] = data_ref[j, 8:16, :].astype(jnp.bfloat16)
        return carry

    lax.fori_loop(0, blocks, prepare, 0)
    sum_ref[...] = jnp.zeros_like(sum_ref)

    def over_cells(left, right):
        return lax.dot_general(left, right, (((1,), (1,)), ((), ())), preferred_element_type=jnp.float32)

    def columns(step):
        return pl.ds(pl.multiple_of(step * CELL_STEP, CELL_STEP), CELL_STEP)

    def fill(step, slot_at, add):
        to = columns(slot_at)
        x = x_ref[:, columns(step)]
        weights = w_ref[:, columns(step)]

        def some(b, carry):
            here = pl.ds(pl.multiple_of(b * SLOT_STEP, SLOT_STEP), SLOT_STEP)
            turns = jnp.dot(slot_ref[here, 0:DEPTH], x, preferred_element_type=jnp.float32)
            c, s = cos_sin(turns)
            c, s = c.astype(jnp.bfloat16), s.astype(jnp.bfloat16)
            cos_ref[here, to] = c
            sin_ref[here, to] = s
            return carry

        lax.fori_loop(0, slot_steps, some, 0)
        if add and not keep:
            sum_ref[0:8, :] += over_cells(weights, cos_ref[:, to])
            sum_ref[8:16, :] += over_cells(weights, sin_ref[:, to])
        return to

    def forward(step, carry):
        fill(step, step if keep else 0, True)
        return carry

    lax.fori_loop(0, cell_steps, forward, 0)
    if keep:

        def total(b, carry):
            here = pl.ds(pl.multiple_of(b * SLOT_STEP, SLOT_STEP), SLOT_STEP)
            sum_ref[0:8, here] = over_cells(w_ref[...], cos_ref[here, :])
            sum_ref[8:16, here] = over_cells(w_ref[...], sin_ref[here, :])
            return carry

        lax.fori_loop(0, slot_steps, total, 0)
    real, imag = sum_ref[0:8, :] * (norm * COS_UNIT), sum_ref[8:16, :] * (norm * SIN_UNIT)
    ar, br, cr = (real[:, p * width : (p + 1) * width] for p in range(3))
    ai, bi, ci = (imag[:, p * width : (p + 1) * width] for p in range(3))
    cot = cot_ref[...]
    bcr, bci = br * cr - bi * ci, br * ci + bi * cr
    corr_ref[...] = ar * bcr - ai * bci
    acr, aci = ar * cr - ai * ci, ar * ci + ai * cr
    abr, abi = ar * br - ai * bi, ar * bi + ai * br
    scaled_real, scaled_imag = cot * (norm * COS_UNIT), cot * (-norm * SIN_UNIT)
    left_real = jnp.concatenate([scaled_real * t for t in (bcr, acr, abr)], axis=1).astype(jnp.bfloat16)
    left_imag = jnp.concatenate([scaled_imag * t for t in (bci, aci, abi)], axis=1).astype(jnp.bfloat16)

    def backward(step, carry):
        to = columns(step) if keep else fill(step, 0, False)
        out = jnp.dot(left_real, cos_ref[:, to], preferred_element_type=jnp.float32) + jnp.dot(
            left_imag, sin_ref[:, to], preferred_element_type=jnp.float32
        )
        for i in range(per_step):
            grad_ref[step * per_step + i] = out[:, i * LANES : (i + 1) * LANES]
        return carry

    lax.fori_loop(0, cell_steps, backward, 0)


def lookup(triplets, momenta):
    units = jnp.array([1, 32, 1024], jnp.int32)[:, None]
    codes = jnp.sum((momenta - 1) * units, axis=0)
    slots = 3 * triplets.shape[1]
    return pl.pallas_call(
        lookup_kernel, out_shape=jax.ShapeDtypeStruct((slots, LANES), jnp.bfloat16), name="lookup"
    )(triplets, codes.reshape(-1, WIDE))


def triplet_stage(data, slot_rows, cotangent):
    blocks = data.shape[0]
    slots = slot_rows.shape[0]
    cells = blocks * LANES
    keep = 4 * slots * cells <= KEEP_BYTES
    kept = cells if keep else CELL_STEP
    return pl.pallas_call(
        functools.partial(main_kernel, keep, 1.0 / math.sqrt(cells)),
        out_shape=(
            jax.ShapeDtypeStruct(cotangent.shape, jnp.float32),
            jax.ShapeDtypeStruct((blocks, 8, LANES), jnp.float32),
        ),
        scratch_shapes=[
            pltpu.VMEM((DEPTH, cells), jnp.bfloat16),
            pltpu.VMEM((8, cells), jnp.bfloat16),
            pltpu.VMEM((16, slots), jnp.float32),
            pltpu.VMEM((slots, kept), jnp.bfloat16),
            pltpu.VMEM((slots, kept), jnp.bfloat16),
        ],
        in_specs=[pl.BlockSpec(memory_space=pltpu.VMEM)] * 3,
        name="triplet_stage",
    )(data, slot_rows, cotangent)


def gather_cells(block, devices):
    return lax.all_to_all(jnp.broadcast_to(block[None], (devices,) + block.shape), "cell", 0, 0)


def reduce_cells(blocks):
    return lax.all_to_all(blocks, "cell", 0, 0).sum(0)


def on_device(momenta, positions, weights, triplets, cotangent):
    devices = lax.axis_size("cell")
    block = jnp.concatenate(
        [positions, jnp.zeros((5, positions.shape[1]), jnp.float32), weights.astype(jnp.float32)], axis=0
    )
    data = gather_cells(block, devices)
    slot_rows = lookup(triplets, momenta)
    correlation, partial = triplet_stage(data, slot_rows, cotangent)
    return correlation, reduce_cells(partial)


def solution(mesh):
    split = P(None, ("grp", "cell"))
    return jax.shard_map(
        on_device,
        mesh=mesh,
        in_specs=(P(), split, split, split, split),
        out_specs=(split, split),
        check_vma=False,
    )
```

```python
import functools
import math

import jax
import jax.numpy as jnp
import numpy as np
from jax import lax
from jax.experimental import pallas as pl
from jax.experimental.pallas import tpu as pltpu
from jax.sharding import PartitionSpec as P

LANES = 128
WIDE = 256
ROWS = 16
DEPTH = 32
CELL_STEP = 512
SLOT_STEP = 1536
SUM_STEP = 1536
BACK_STEP = 2048
KEEP_BYTES = 24 << 20


def fit(values, terms):
    nodes = 0.125 + 0.125 * np.cos(np.pi * (np.arange(64) + 0.5) / 64)
    series = np.polynomial.chebyshev.Chebyshev.fit(nodes, values(np.sqrt(nodes)), terms - 1, domain=[0.0, 0.25])
    all_of = series.convert(kind=np.polynomial.Polynomial).coef
    return [float(c / all_of[-1]) for c in all_of[:-1]], float(all_of[-1])


SINE, SINE_TOP = fit(lambda f: np.sin(0.5 * np.pi * f) / f, 3)
COSINE, COSINE_TOP = fit(lambda f: np.cos(0.5 * np.pi * f), 4)
HALF_COSINE = 2.0 * SINE_TOP * SINE_TOP
COS_UNIT = 2.0 ** round(math.log2(8.0 * (SINE_TOP * COSINE_TOP) ** 2))
HALF_SINE = math.sqrt(0.5 * COS_UNIT)
RATIO = 2.0 * SINE_TOP * COSINE_TOP / HALF_SINE
SIN_UNIT = 2.0 * HALF_SINE * HALF_COSINE


def series_of(u, top, coefficients):
    total = (u if top == 1.0 else top * u) + coefficients[-1]
    for c in coefficients[-2::-1]:
        total = total * u + c
    return total


def cos_sin(turns):
    f = turns - jnp.round(turns)
    u = f * f
    s = f * series_of(u, 1.0, SINE)
    c = series_of(u, RATIO, [RATIO * v for v in COSINE])
    half = s * c
    return 1.0 / COS_UNIT - half * half, half * (1.0 / HALF_COSINE - s * s)


def lookup_kernel(tri_ref, table_ref, out_ref):
    rows = table_ref.shape[0]
    width = tri_ref.shape[1]
    lane_iota = lax.broadcasted_iota(jnp.int32, (WIDE, width), 0)
    row_iota = lax.broadcasted_iota(jnp.int32, (rows, width), 0)
    table = table_ref[...]
    bytes_of = jnp.concatenate([table & 255, table - (table & 255)], axis=1)
    left = bytes_of.astype(jnp.float32).astype(jnp.bfloat16)
    for place in range(3):
        index = tri_ref[place : place + 1, :]
        pick = jnp.where(lane_iota == (index & (WIDE - 1)), 1.0, 0.0).astype(jnp.bfloat16)
        line = jnp.dot(left, jnp.concatenate([pick, pick], axis=0), preferred_element_type=jnp.float32)
        code = jnp.sum(jnp.where(row_iota == (index >> (WIDE.bit_length() - 1)), line, 0.0), axis=0, keepdims=True)
        third = jnp.floor(code * (1.0 / 1024.0))
        rest = code - 1024.0 * third
        second = jnp.floor(rest * (1.0 / 32.0))
        first = rest - 32.0 * second
        eight = jnp.concatenate([first + 1.0, second + 1.0, third + 1.0, jnp.zeros((5, width), jnp.float32)], axis=0)
        wide = jnp.concatenate([eight, eight, eight, jnp.zeros((LANES - 24, width), jnp.float32)], axis=0)
        out_ref[place * width : (place + 1) * width, :] = wide.T.astype(jnp.bfloat16)


def main_kernel(keep, norm, data_ref, slot_ref, cot_ref, corr_ref, grad_ref, x_ref, w_ref, sum_ref, cos_ref, sin_ref):
    blocks = data_ref.shape[0]
    slots = slot_ref.shape[0]
    width = cot_ref.shape[1]
    cells = blocks * LANES
    cell_steps = cells // CELL_STEP
    slot_step = math.gcd(SLOT_STEP, slots)
    sum_step = math.gcd(SUM_STEP, slots)
    slot_steps = slots // slot_step

    def prepare(j, carry):
        at = pl.ds(pl.multiple_of(j * LANES, LANES), LANES)
        place = data_ref[j, 0:8, :]
        place = place - jnp.round(place)
        high = place.astype(jnp.bfloat16).astype(jnp.float32)
        rest = place - high
        middle = rest.astype(jnp.bfloat16).astype(jnp.float32)
        low = rest - middle
        none = jnp.zeros_like(low)
        x_ref[:, at] = jnp.concatenate([high, middle, low, none], axis=0).astype(jnp.bfloat16)
        w_ref[:, at] = data_ref[j, 8:16, :].astype(jnp.bfloat16)
        return carry

    lax.fori_loop(0, blocks, prepare, 0)
    sum_ref[...] = jnp.zeros_like(sum_ref)

    def over_cells(left, right):
        return lax.dot_general(left, right, (((1,), (1,)), ((), ())), preferred_element_type=jnp.float32)

    def columns(step):
        return pl.ds(pl.multiple_of(step * CELL_STEP, CELL_STEP), CELL_STEP)

    def fill(step, slot_at, add):
        to = columns(slot_at)
        x = x_ref[:, columns(step)]
        weights = w_ref[:, columns(step)]

        def some(b, carry):
            here = pl.ds(pl.multiple_of(b * slot_step, slot_step), slot_step)
            turns = jnp.dot(slot_ref[here, 0:DEPTH], x, preferred_element_type=jnp.float32)
            c, s = cos_sin(turns)
            c, s = c.astype(jnp.bfloat16), s.astype(jnp.bfloat16)
            cos_ref[here, to] = c
            sin_ref[here, to] = s
            return carry

        lax.fori_loop(0, slot_steps, some, 0)
        if add and not keep:
            sum_ref[0:8, :] += over_cells(weights, cos_ref[:, to])
            sum_ref[8:16, :] += over_cells(weights, sin_ref[:, to])
        return to

    def forward(step, carry):
        fill(step, step if keep else 0, True)
        return carry

    lax.fori_loop(0, cell_steps, forward, 0)
    if keep:

        def total(b, carry):
            here = pl.ds(pl.multiple_of(b * sum_step, sum_step), sum_step)
            sum_ref[0:8, here] = over_cells(w_ref[...], cos_ref[here, :])
            sum_ref[8:16, here] = over_cells(w_ref[...], sin_ref[here, :])
            return carry

        lax.fori_loop(0, slots // sum_step, total, 0)
    real, imag = sum_ref[0:8, :] * (norm * COS_UNIT), sum_ref[8:16, :] * (norm * SIN_UNIT)
    ar, br, cr = (real[:, p * width : (p + 1) * width] for p in range(3))
    ai, bi, ci = (imag[:, p * width : (p + 1) * width] for p in range(3))
    cot = cot_ref[...]
    bcr, bci = br * cr - bi * ci, br * ci + bi * cr
    corr_ref[...] = ar * bcr - ai * bci
    acr, aci = ar * cr - ai * ci, ar * ci + ai * cr
    abr, abi = ar * br - ai * bi, ar * bi + ai * br
    scaled_real, scaled_imag = cot * (norm * COS_UNIT), cot * (-norm * SIN_UNIT)
    left_real = jnp.concatenate([scaled_real * t for t in (bcr, acr, abr)], axis=1).astype(jnp.bfloat16)
    left_imag = jnp.concatenate([scaled_imag * t for t in (bci, aci, abi)], axis=1).astype(jnp.bfloat16)

    back_step = math.gcd(BACK_STEP, cells) if keep else CELL_STEP
    per_step = back_step // LANES

    def backward(step, carry):
        to = pl.ds(pl.multiple_of(step * back_step, back_step), back_step) if keep else fill(step, 0, False)
        out = jnp.dot(left_real, cos_ref[:, to], preferred_element_type=jnp.float32) + jnp.dot(
            left_imag, sin_ref[:, to], preferred_element_type=jnp.float32
        )
        for i in range(per_step):
            grad_ref[step * per_step + i] = out[:, i * LANES : (i + 1) * LANES]
        return carry

    lax.fori_loop(0, cells // back_step, backward, 0)


def lookup(triplets, momenta):
    units = jnp.array([1, 32, 1024], jnp.int32)[:, None]
    codes = jnp.sum((momenta - 1) * units, axis=0)
    slots = 3 * triplets.shape[1]
    return pl.pallas_call(
        lookup_kernel, out_shape=jax.ShapeDtypeStruct((slots, LANES), jnp.bfloat16), name="lookup"
    )(triplets, codes.reshape(-1, WIDE))


def triplet_stage(data, slot_rows, cotangent):
    blocks = data.shape[0]
    slots = slot_rows.shape[0]
    cells = blocks * LANES
    keep = 4 * slots * cells <= KEEP_BYTES
    kept = cells if keep else CELL_STEP
    return pl.pallas_call(
        functools.partial(main_kernel, keep, 1.0 / math.sqrt(cells)),
        out_shape=(
            jax.ShapeDtypeStruct(cotangent.shape, jnp.float32),
            jax.ShapeDtypeStruct((blocks, 8, LANES), jnp.float32),
        ),
        scratch_shapes=[
            pltpu.VMEM((DEPTH, cells), jnp.bfloat16),
            pltpu.VMEM((8, cells), jnp.bfloat16),
            pltpu.VMEM((16, slots), jnp.float32),
            pltpu.VMEM((slots, kept), jnp.bfloat16),
            pltpu.VMEM((slots, kept), jnp.bfloat16),
        ],
        in_specs=[pl.BlockSpec(memory_space=pltpu.VMEM)] * 3,
        name="triplet_stage",
    )(data, slot_rows, cotangent)


def reduce_cells(blocks):
    return lax.all_to_all(blocks, "cell", 0, 0).sum(0)


def pack_kernel(place_ref, weight_ref, out_ref):
    width = place_ref.shape[1]
    block = jnp.concatenate(
        [place_ref[...], jnp.zeros((5, width), jnp.float32), weight_ref[...].astype(jnp.float32)], axis=0
    )
    for i in range(out_ref.shape[0]):
        out_ref[i] = block


def pack(positions, weights, devices):
    return pl.pallas_call(
        pack_kernel, out_shape=jax.ShapeDtypeStruct((devices, ROWS, positions.shape[1]), jnp.float32), name="pack"
    )(positions, weights)


def on_device(momenta, positions, weights, triplets, cotangent):
    devices = lax.axis_size("cell")
    data = lax.all_to_all(pack(positions, weights, devices), "cell", 0, 0)
    data = pltpu.with_memory_space_constraint(data, pltpu.VMEM)
    slot_rows = lookup(triplets, momenta)
    correlation, partial = triplet_stage(data, slot_rows, cotangent)
    return correlation, reduce_cells(partial)


def solution(mesh):
    split = P(None, ("grp", "cell"))
    return jax.shard_map(
        on_device,
        mesh=mesh,
        in_specs=(P(), split, split, split, split),
        out_specs=(split, split),
        check_vma=False,
    )
```

```python
import functools
import math

import jax
import jax.numpy as jnp
import numpy as np
from jax import lax
from jax.experimental import pallas as pl
from jax.experimental.pallas import tpu as pltpu
from jax.sharding import PartitionSpec as P

LANES = 128
WIDE = 256
DEPTH = 16
ROWS = 24
CELL_STEP = 2048
SLOT_STEP = 1536
BACK_STEP = 2048
KEEP_BYTES = 24 << 20


def fit(values, terms):
    nodes = 0.125 + 0.125 * np.cos(np.pi * (np.arange(64) + 0.5) / 64)
    series = np.polynomial.chebyshev.Chebyshev.fit(nodes, values(np.sqrt(nodes)), terms - 1, domain=[0.0, 0.25])
    all_of = series.convert(kind=np.polynomial.Polynomial).coef
    return [float(c / all_of[-1]) for c in all_of[:-1]], float(all_of[-1])


SINE, SINE_TOP = fit(lambda f: np.sin(0.5 * np.pi * f) / f, 3)
COSINE, COSINE_TOP = fit(lambda f: np.cos(0.5 * np.pi * f), 4)
HALF_COSINE = 2.0 * SINE_TOP * SINE_TOP
COS_UNIT = 2.0 ** round(math.log2(8.0 * (SINE_TOP * COSINE_TOP) ** 2))
HALF_SINE = math.sqrt(0.5 * COS_UNIT)
RATIO = 2.0 * SINE_TOP * COSINE_TOP / HALF_SINE
SIN_UNIT = 2.0 * HALF_SINE * HALF_COSINE


def series_of(u, top, coefficients):
    total = (u if top == 1.0 else top * u) + coefficients[-1]
    for c in coefficients[-2::-1]:
        total = total * u + c
    return total


def cos_sin(turns):
    f = turns - jnp.round(turns)
    u = f * f
    s = f * series_of(u, 1.0, SINE)
    c = series_of(u, RATIO, [RATIO * v for v in COSINE])
    half = s * c
    return 1.0 / COS_UNIT - half * half, half * (1.0 / HALF_COSINE - s * s)


def lookup_kernel(tri_ref, table_ref, out_ref):
    rows = table_ref.shape[0]
    width = tri_ref.shape[1]
    lane_iota = lax.broadcasted_iota(jnp.int32, (WIDE, width), 0)
    row_iota = lax.broadcasted_iota(jnp.int32, (rows, width), 0)
    table = table_ref[...]
    bytes_of = jnp.concatenate([table & 255, table - (table & 255)], axis=1)
    left = bytes_of.astype(jnp.float32).astype(jnp.bfloat16)
    for place in range(3):
        index = tri_ref[place : place + 1, :]
        pick = jnp.where(lane_iota == (index & (WIDE - 1)), 1.0, 0.0).astype(jnp.bfloat16)
        line = jnp.dot(left, jnp.concatenate([pick, pick], axis=0), preferred_element_type=jnp.float32)
        code = jnp.sum(jnp.where(row_iota == (index >> (WIDE.bit_length() - 1)), line, 0.0), axis=0, keepdims=True)
        third = jnp.floor(code * (1.0 / 1024.0))
        rest = code - 1024.0 * third
        second = jnp.floor(rest * (1.0 / 32.0))
        first = rest - 32.0 * second
        three = [first + 1.0, second + 1.0, third + 1.0]
        wide = jnp.concatenate(three * 3 + [jnp.zeros((LANES - 9, width), jnp.float32)], axis=0)
        out_ref[place * width : (place + 1) * width, :] = wide.T.astype(jnp.bfloat16)


def main_kernel(keep, norm, data_ref, slot_ref, cot_ref, corr_ref, grad_ref, x_ref, w_ref, sum_ref, cos_ref, sin_ref):
    blocks = data_ref.shape[0]
    slots = slot_ref.shape[0]
    width = cot_ref.shape[1]
    cells = blocks * LANES
    cell_step = math.gcd(CELL_STEP, cells)
    cell_steps = cells // cell_step
    slot_step = math.gcd(SLOT_STEP, slots)
    slot_steps = slots // slot_step

    def prepare(j, carry):
        at = pl.ds(pl.multiple_of(j * LANES, LANES), LANES)
        x_ref[:, at] = data_ref[j, 0:DEPTH, :]
        w_ref[:, at] = data_ref[j, DEPTH:ROWS, :]
        return carry

    lax.fori_loop(0, blocks, prepare, 0)
    sum_ref[...] = jnp.zeros_like(sum_ref)

    def over_cells(left, right):
        return lax.dot_general(left, right, (((1,), (1,)), ((), ())), preferred_element_type=jnp.float32)

    def columns(step):
        return pl.ds(pl.multiple_of(step * cell_step, cell_step), cell_step)

    def fill(step, slot_at, add):
        to = columns(slot_at)
        x = x_ref[:, columns(step)]
        weights = w_ref[:, columns(step)]

        def some(b, carry):
            here = pl.ds(pl.multiple_of(b * slot_step, slot_step), slot_step)
            turns = jnp.dot(slot_ref[here, 0:DEPTH], x, preferred_element_type=jnp.float32)
            c, s = cos_sin(turns)
            c, s = c.astype(jnp.bfloat16), s.astype(jnp.bfloat16)
            cos_ref[here, to] = c
            sin_ref[here, to] = s
            if add:
                sum_ref[0:8, here] += over_cells(weights, c)
                sum_ref[8:16, here] += over_cells(weights, s)
            return carry

        lax.fori_loop(0, slot_steps, some, 0)
        return to

    def forward(step, carry):
        fill(step, step if keep else 0, True)
        return carry

    lax.fori_loop(0, cell_steps, forward, 0)
    real, imag = sum_ref[0:8, :] * (norm * COS_UNIT), sum_ref[8:16, :] * (norm * SIN_UNIT)
    ar, br, cr = (real[:, p * width : (p + 1) * width] for p in range(3))
    ai, bi, ci = (imag[:, p * width : (p + 1) * width] for p in range(3))
    cot = cot_ref[...]
    bcr, bci = br * cr - bi * ci, br * ci + bi * cr
    corr_ref[...] = ar * bcr - ai * bci
    acr, aci = ar * cr - ai * ci, ar * ci + ai * cr
    abr, abi = ar * br - ai * bi, ar * bi + ai * br
    scaled_real, scaled_imag = cot * (norm * COS_UNIT), cot * (-norm * SIN_UNIT)
    left_real = jnp.concatenate([scaled_real * t for t in (bcr, acr, abr)], axis=1).astype(jnp.bfloat16)
    left_imag = jnp.concatenate([scaled_imag * t for t in (bci, aci, abi)], axis=1).astype(jnp.bfloat16)

    back_step = math.gcd(BACK_STEP, cells) if keep else cell_step
    per_step = back_step // LANES

    def backward(step, carry):
        to = pl.ds(pl.multiple_of(step * back_step, back_step), back_step) if keep else fill(step, 0, False)
        out = jnp.dot(left_real, cos_ref[:, to], preferred_element_type=jnp.float32) + jnp.dot(
            left_imag, sin_ref[:, to], preferred_element_type=jnp.float32
        )
        for i in range(per_step):
            grad_ref[step * per_step + i] = out[:, i * LANES : (i + 1) * LANES]
        return carry

    lax.fori_loop(0, cells // back_step, backward, 0)


def lookup(triplets, momenta):
    units = jnp.array([1, 32, 1024], jnp.int32)[:, None]
    codes = jnp.sum((momenta - 1) * units, axis=0)
    slots = 3 * triplets.shape[1]
    return pl.pallas_call(
        lookup_kernel, out_shape=jax.ShapeDtypeStruct((slots, LANES), jnp.bfloat16), name="lookup"
    )(triplets, codes.reshape(-1, WIDE))


def triplet_stage(data, slot_rows, cotangent):
    blocks = data.shape[0]
    slots = slot_rows.shape[0]
    cells = blocks * LANES
    keep = 4 * slots * cells <= KEEP_BYTES
    kept = cells if keep else math.gcd(CELL_STEP, cells)
    return pl.pallas_call(
        functools.partial(main_kernel, keep, 1.0 / math.sqrt(cells)),
        out_shape=(
            jax.ShapeDtypeStruct(cotangent.shape, jnp.float32),
            jax.ShapeDtypeStruct((blocks, 8, LANES), jnp.float32),
        ),
        scratch_shapes=[
            pltpu.VMEM((DEPTH, cells), jnp.bfloat16),
            pltpu.VMEM((8, cells), jnp.bfloat16),
            pltpu.VMEM((16, slots), jnp.float32),
            pltpu.VMEM((slots, kept), jnp.bfloat16),
            pltpu.VMEM((slots, kept), jnp.bfloat16),
        ],
        in_specs=[pl.BlockSpec(memory_space=pltpu.VMEM)] * 3,
        name="triplet_stage",
    )(data, slot_rows, cotangent)


def reduce_cells(blocks):
    return lax.all_to_all(blocks, "cell", 0, 0).sum(0)


def pack_kernel(place_ref, weight_ref, out_ref):
    place = place_ref[...]
    place = place - jnp.round(place)
    high = place.astype(jnp.bfloat16).astype(jnp.float32)
    rest = place - high
    middle = rest.astype(jnp.bfloat16).astype(jnp.float32)
    none = jnp.zeros((DEPTH - 9, place.shape[1]), jnp.float32)
    rows = [high, middle, rest - middle, none, weight_ref[...].astype(jnp.float32)]
    block = jnp.concatenate(rows, axis=0).astype(jnp.bfloat16)
    for i in range(out_ref.shape[0]):
        out_ref[i] = block


def pack(positions, weights, devices):
    return pl.pallas_call(
        pack_kernel, out_shape=jax.ShapeDtypeStruct((devices, ROWS, positions.shape[1]), jnp.bfloat16), name="pack"
    )(positions, weights)


def on_device(momenta, positions, weights, triplets, cotangent):
    devices = lax.axis_size("cell")
    data = lax.all_to_all(pack(positions, weights, devices), "cell", 0, 0)
    data = pltpu.with_memory_space_constraint(data, pltpu.VMEM)
    slot_rows = lookup(triplets, momenta)
    correlation, partial = triplet_stage(data, slot_rows, cotangent)
    return correlation, reduce_cells(partial)


def solution(mesh):
    split = P(None, ("grp", "cell"))
    return jax.shard_map(
        on_device,
        mesh=mesh,
        in_specs=(P(), split, split, split, split),
        out_specs=(split, split),
        check_vma=False,
    )
```

```python
import functools
import math

import jax
import jax.numpy as jnp
import numpy as np
from jax import lax
from jax.experimental import pallas as pl
from jax.experimental.pallas import tpu as pltpu
from jax.sharding import PartitionSpec as P

LANES = 128
WIDE = 256
DEPTH = 16
ROWS = 24
CELL_STEP = 2048
SLOT_STEP = 1536
BACK_STEP = 2048
KEEP_BYTES = 24 << 20


def fit(values, terms):
    nodes = 0.125 + 0.125 * np.cos(np.pi * (np.arange(64) + 0.5) / 64)
    series = np.polynomial.chebyshev.Chebyshev.fit(nodes, values(np.sqrt(nodes)), terms - 1, domain=[0.0, 0.25])
    all_of = series.convert(kind=np.polynomial.Polynomial).coef
    return [float(c / all_of[-1]) for c in all_of[:-1]], float(all_of[-1])


SINE, SINE_TOP = fit(lambda f: np.sin(0.5 * np.pi * f) / f, 3)
COSINE, COSINE_TOP = fit(lambda f: np.cos(0.5 * np.pi * f), 4)
HALF_COSINE = 2.0 * SINE_TOP * SINE_TOP
COS_UNIT = 2.0 ** round(math.log2(8.0 * (SINE_TOP * COSINE_TOP) ** 2))
HALF_SINE = math.sqrt(0.5 * COS_UNIT)
RATIO = 2.0 * SINE_TOP * COSINE_TOP / HALF_SINE
SIN_UNIT = 2.0 * HALF_SINE * HALF_COSINE


def series_of(u, top, coefficients):
    total = (u if top == 1.0 else top * u) + coefficients[-1]
    for c in coefficients[-2::-1]:
        total = total * u + c
    return total


def cos_sin(turns):
    f = turns - jnp.round(turns)
    u = f * f
    s = f * series_of(u, 1.0, SINE)
    c = series_of(u, RATIO, [RATIO * v for v in COSINE])
    half = s * c
    return 1.0 / COS_UNIT - half * half, half * (1.0 / HALF_COSINE - s * s)


def lookup_kernel(tri_ref, table_ref, out_ref):
    rows = table_ref.shape[0]
    width = tri_ref.shape[1]
    lane_iota = lax.broadcasted_iota(jnp.int32, (WIDE, width), 0)
    row_iota = lax.broadcasted_iota(jnp.int32, (rows, width), 0)
    table = table_ref[...]
    bytes_of = jnp.concatenate([table & 255, table - (table & 255)], axis=1)
    left = bytes_of.astype(jnp.float32).astype(jnp.bfloat16)
    for place in range(3):
        index = tri_ref[place : place + 1, :]
        pick = jnp.where(lane_iota == (index & (WIDE - 1)), 1.0, 0.0).astype(jnp.bfloat16)
        line = jnp.dot(left, jnp.concatenate([pick, pick], axis=0), preferred_element_type=jnp.float32)
        code = jnp.sum(jnp.where(row_iota == (index >> (WIDE.bit_length() - 1)), line, 0.0), axis=0, keepdims=True)
        third = jnp.floor(code * (1.0 / 1024.0))
        rest = code - 1024.0 * third
        second = jnp.floor(rest * (1.0 / 32.0))
        first = rest - 32.0 * second
        three = [first + 1.0, second + 1.0, third + 1.0]
        wide = jnp.concatenate(three * 3 + [jnp.zeros((LANES - 9, width), jnp.float32)], axis=0)
        out_ref[place * width : (place + 1) * width, :] = wide.T.astype(jnp.bfloat16)


def main_kernel(keep, norm, data_ref, slot_ref, cot_ref, corr_ref, grad_ref, x_ref, w_ref, sum_ref, cos_ref, sin_ref):
    blocks = data_ref.shape[0]
    slots = slot_ref.shape[0]
    width = cot_ref.shape[1]
    cells = blocks * LANES
    cell_step = math.gcd(CELL_STEP, cells)
    cell_steps = cells // cell_step
    slot_step = math.gcd(SLOT_STEP, slots)
    slot_steps = slots // slot_step

    def prepare(j, carry):
        at = pl.ds(pl.multiple_of(j * LANES, LANES), LANES)
        x_ref[:, at] = data_ref[j, 0:DEPTH, :]
        w_ref[:, at] = data_ref[j, DEPTH:ROWS, :]
        return carry

    lax.fori_loop(0, blocks, prepare, 0)
    sum_ref[...] = jnp.zeros_like(sum_ref)

    def over_cells(left, right):
        return lax.dot_general(left, right, (((1,), (1,)), ((), ())), preferred_element_type=jnp.float32)

    def columns(step):
        return pl.ds(pl.multiple_of(step * cell_step, cell_step), cell_step)

    def fill(step, slot_at, add):
        to = columns(slot_at)
        x = x_ref[:, columns(step)]
        weights = w_ref[:, columns(step)]

        def some(b, carry):
            here = pl.ds(pl.multiple_of(b * slot_step, slot_step), slot_step)
            turns = jnp.dot(slot_ref[here, 0:DEPTH], x, preferred_element_type=jnp.float32)
            c, s = cos_sin(turns)
            c, s = c.astype(jnp.bfloat16), s.astype(jnp.bfloat16)
            cos_ref[here, to] = c
            sin_ref[here, to] = s
            if add:
                sum_ref[0:8, here] += over_cells(weights, c)
                sum_ref[8:16, here] += over_cells(weights, s)
            return carry

        lax.fori_loop(0, slot_steps, some, 0)
        return to

    def forward(step, carry):
        fill(step, step if keep else 0, True)
        return carry

    lax.fori_loop(0, cell_steps, forward, 0)
    real, imag = sum_ref[0:8, :] * (norm * COS_UNIT), sum_ref[8:16, :] * (norm * SIN_UNIT)
    ar, br, cr = (real[:, p * width : (p + 1) * width] for p in range(3))
    ai, bi, ci = (imag[:, p * width : (p + 1) * width] for p in range(3))
    cot = cot_ref[...]
    bcr, bci = br * cr - bi * ci, br * ci + bi * cr
    corr_ref[...] = ar * bcr - ai * bci
    acr, aci = ar * cr - ai * ci, ar * ci + ai * cr
    abr, abi = ar * br - ai * bi, ar * bi + ai * br
    scaled_real, scaled_imag = cot * (norm * COS_UNIT), cot * (-norm * SIN_UNIT)
    left_real = jnp.concatenate([scaled_real * t for t in (bcr, acr, abr)], axis=1).astype(jnp.bfloat16)
    left_imag = jnp.concatenate([scaled_imag * t for t in (bci, aci, abi)], axis=1).astype(jnp.bfloat16)

    back_step = math.gcd(BACK_STEP, cells) if keep else cell_step
    per_step = back_step // LANES

    def backward(step, carry):
        to = pl.ds(pl.multiple_of(step * back_step, back_step), back_step) if keep else fill(step, 0, False)
        out = jnp.dot(left_real, cos_ref[:, to], preferred_element_type=jnp.float32) + jnp.dot(
            left_imag, sin_ref[:, to], preferred_element_type=jnp.float32
        )
        for i in range(per_step):
            grad_ref[step * per_step + i] = out[:, i * LANES : (i + 1) * LANES]
        return carry

    lax.fori_loop(0, cells // back_step, backward, 0)


def lookup(triplets, momenta):
    units = jnp.array([1, 32, 1024], jnp.int32)[:, None]
    codes = jnp.sum((momenta - 1) * units, axis=0)
    slots = 3 * triplets.shape[1]
    return pl.pallas_call(
        lookup_kernel, out_shape=jax.ShapeDtypeStruct((slots, LANES), jnp.bfloat16), name="lookup"
    )(triplets, codes.reshape(-1, WIDE))


def triplet_stage(data, slot_rows, cotangent):
    blocks = data.shape[0]
    slots = slot_rows.shape[0]
    cells = blocks * LANES
    keep = 4 * slots * cells <= KEEP_BYTES
    kept = cells if keep else math.gcd(CELL_STEP, cells)
    return pl.pallas_call(
        functools.partial(main_kernel, keep, 1.0 / math.sqrt(cells)),
        out_shape=(
            jax.ShapeDtypeStruct(cotangent.shape, jnp.float32),
            pltpu.VMEM((blocks, 8, LANES), jnp.float32),
        ),
        scratch_shapes=[
            pltpu.VMEM((DEPTH, cells), jnp.bfloat16),
            pltpu.VMEM((8, cells), jnp.bfloat16),
            pltpu.VMEM((16, slots), jnp.float32),
            pltpu.VMEM((slots, kept), jnp.bfloat16),
            pltpu.VMEM((slots, kept), jnp.bfloat16),
        ],
        in_specs=[pl.BlockSpec(memory_space=pltpu.VMEM)] * 3,
        name="triplet_stage",
    )(data, slot_rows, cotangent)


def reduce_cells(blocks):
    return lax.all_to_all(blocks, "cell", 0, 0).sum(0)


def pack_kernel(place_ref, weight_ref, out_ref):
    place = place_ref[...]
    place = place - jnp.round(place)
    high = place.astype(jnp.bfloat16).astype(jnp.float32)
    rest = place - high
    middle = rest.astype(jnp.bfloat16).astype(jnp.float32)
    none = jnp.zeros((DEPTH - 9, place.shape[1]), jnp.float32)
    rows = [high, middle, rest - middle, none, weight_ref[...].astype(jnp.float32)]
    block = jnp.concatenate(rows, axis=0).astype(jnp.bfloat16)
    for i in range(out_ref.shape[0]):
        out_ref[i] = block


def pack(positions, weights, devices):
    return pl.pallas_call(
        pack_kernel, out_shape=jax.ShapeDtypeStruct((devices, ROWS, positions.shape[1]), jnp.bfloat16), name="pack"
    )(positions, weights)


def on_device(momenta, positions, weights, triplets, cotangent):
    devices = lax.axis_size("cell")
    data = lax.all_to_all(pack(positions, weights, devices), "cell", 0, 0)
    data = pltpu.with_memory_space_constraint(data, pltpu.VMEM)
    slot_rows = lookup(triplets, momenta)
    correlation, partial = triplet_stage(data, slot_rows, cotangent)
    return correlation, reduce_cells(partial)


def solution(mesh):
    split = P(None, ("grp", "cell"))
    return jax.shard_map(
        on_device,
        mesh=mesh,
        in_specs=(P(), split, split, split, split),
        out_specs=(split, split),
        check_vma=False,
    )
```

```python
import functools
import math

import jax
import jax.numpy as jnp
import numpy as np
from jax import lax
from jax.experimental import pallas as pl
from jax.experimental.pallas import tpu as pltpu
from jax.sharding import PartitionSpec as P

LANES = 128
WIDE = 256
DEPTH = 16
ROWS = 24
CELL_STEP = 2048
SLOT_STEP = 1536
BACK_STEP = 2048
KEEP_BYTES = 24 << 20


def fit(values, terms):
    nodes = 0.125 + 0.125 * np.cos(np.pi * (np.arange(64) + 0.5) / 64)
    series = np.polynomial.chebyshev.Chebyshev.fit(nodes, values(np.sqrt(nodes)), terms - 1, domain=[0.0, 0.25])
    all_of = series.convert(kind=np.polynomial.Polynomial).coef
    return [float(c / all_of[-1]) for c in all_of[:-1]], float(all_of[-1])


SINE, SINE_TOP = fit(lambda f: np.sin(0.5 * np.pi * f) / f, 3)
COSINE, COSINE_TOP = fit(lambda f: np.cos(0.5 * np.pi * f), 4)
HALF_COSINE = 2.0 * SINE_TOP * SINE_TOP
COS_UNIT = 2.0 ** round(math.log2(8.0 * (SINE_TOP * COSINE_TOP) ** 2))
HALF_SINE = math.sqrt(0.5 * COS_UNIT)
RATIO = 2.0 * SINE_TOP * COSINE_TOP / HALF_SINE
SIN_UNIT = 2.0 * HALF_SINE * HALF_COSINE


def series_of(u, top, coefficients):
    total = (u if top == 1.0 else top * u) + coefficients[-1]
    for c in coefficients[-2::-1]:
        total = total * u + c
    return total


def cos_sin(turns):
    f = turns - jnp.round(turns)
    u = f * f
    s = f * series_of(u, 1.0, SINE)
    c = series_of(u, RATIO, [RATIO * v for v in COSINE])
    half = s * c
    return 1.0 / COS_UNIT - half * half, half * (1.0 / HALF_COSINE - s * s)


def lookup_kernel(tri_ref, table_ref, out_ref):
    rows = table_ref.shape[0]
    width = tri_ref.shape[1]
    lane_iota = lax.broadcasted_iota(jnp.int32, (WIDE, width), 0)
    row_iota = lax.broadcasted_iota(jnp.int32, (rows, width), 0)
    table = table_ref[...]
    bytes_of = jnp.concatenate([table & 255, table - (table & 255)], axis=1)
    left = bytes_of.astype(jnp.float32).astype(jnp.bfloat16)
    for place in range(3):
        index = tri_ref[place : place + 1, :]
        pick = jnp.where(lane_iota == (index & (WIDE - 1)), 1.0, 0.0).astype(jnp.bfloat16)
        line = jnp.dot(left, jnp.concatenate([pick, pick], axis=0), preferred_element_type=jnp.float32)
        code = jnp.sum(jnp.where(row_iota == (index >> (WIDE.bit_length() - 1)), line, 0.0), axis=0, keepdims=True)
        third = jnp.floor(code * (1.0 / 1024.0))
        rest = code - 1024.0 * third
        second = jnp.floor(rest * (1.0 / 32.0))
        first = rest - 32.0 * second
        three = [first + 1.0, second + 1.0, third + 1.0]
        wide = jnp.concatenate(three * 3 + [jnp.zeros((LANES - 9, width), jnp.float32)], axis=0)
        out_ref[place * width : (place + 1) * width, :] = wide.T.astype(jnp.bfloat16)


def main_kernel(keep, norm, data_ref, slot_ref, cot_ref, corr_ref, grad_ref, x_ref, w_ref, sum_ref, cos_ref, sin_ref):
    blocks = data_ref.shape[0]
    slots = slot_ref.shape[0]
    width = cot_ref.shape[1]
    cells = blocks * LANES
    cell_step = math.gcd(CELL_STEP, cells)
    cell_steps = cells // cell_step
    slot_step = math.gcd(SLOT_STEP, slots)
    slot_steps = slots // slot_step

    def prepare(j, carry):
        at = pl.ds(pl.multiple_of(j * LANES, LANES), LANES)
        x_ref[:, at] = data_ref[j, 0:DEPTH, :]
        w_ref[:, at] = data_ref[j, DEPTH:ROWS, :]
        return carry

    lax.fori_loop(0, blocks, prepare, 0)
    sum_ref[...] = jnp.zeros_like(sum_ref)

    def over_cells(left, right):
        return lax.dot_general(left, right, (((1,), (1,)), ((), ())), preferred_element_type=jnp.float32)

    def columns(step):
        return pl.ds(pl.multiple_of(step * cell_step, cell_step), cell_step)

    def fill(step, slot_at, add):
        to = columns(slot_at)
        x = x_ref[:, columns(step)]
        weights = w_ref[:, columns(step)]

        def some(b, carry):
            here = pl.ds(pl.multiple_of(b * slot_step, slot_step), slot_step)
            turns = jnp.dot(slot_ref[here, 0:DEPTH], x, preferred_element_type=jnp.float32)
            c, s = cos_sin(turns)
            c, s = c.astype(jnp.bfloat16), s.astype(jnp.bfloat16)
            cos_ref[here, to] = c
            sin_ref[here, to] = s
            if add:
                sum_ref[0:8, here] += over_cells(weights, c)
                sum_ref[8:16, here] += over_cells(weights, s)
            return carry

        lax.fori_loop(0, slot_steps, some, 0)
        return to

    def forward(step, carry):
        fill(step, step if keep else 0, True)
        return carry

    lax.fori_loop(0, cell_steps, forward, 0)
    real, imag = sum_ref[0:8, :] * (norm * COS_UNIT), sum_ref[8:16, :] * (norm * SIN_UNIT)
    ar, br, cr = (real[:, p * width : (p + 1) * width] for p in range(3))
    ai, bi, ci = (imag[:, p * width : (p + 1) * width] for p in range(3))
    cot = cot_ref[...]
    bcr, bci = br * cr - bi * ci, br * ci + bi * cr
    corr_ref[...] = ar * bcr - ai * bci
    acr, aci = ar * cr - ai * ci, ar * ci + ai * cr
    abr, abi = ar * br - ai * bi, ar * bi + ai * br
    scaled_real, scaled_imag = cot * (norm * COS_UNIT), cot * (-norm * SIN_UNIT)
    left_real = jnp.concatenate([scaled_real * t for t in (bcr, acr, abr)], axis=1).astype(jnp.bfloat16)
    left_imag = jnp.concatenate([scaled_imag * t for t in (bci, aci, abi)], axis=1).astype(jnp.bfloat16)

    back_step = math.gcd(BACK_STEP, cells) if keep else cell_step
    per_step = back_step // LANES

    def backward(step, carry):
        to = pl.ds(pl.multiple_of(step * back_step, back_step), back_step) if keep else fill(step, 0, False)
        out = jnp.dot(left_real, cos_ref[:, to], preferred_element_type=jnp.float32) + jnp.dot(
            left_imag, sin_ref[:, to], preferred_element_type=jnp.float32
        )
        for i in range(per_step):
            grad_ref[step * per_step + i] = out[:, i * LANES : (i + 1) * LANES]
        return carry

    lax.fori_loop(0, cells // back_step, backward, 0)


def lookup(triplets, momenta):
    units = jnp.array([1, 32, 1024], jnp.int32)[:, None]
    codes = jnp.sum((momenta - 1) * units, axis=0)
    slots = 3 * triplets.shape[1]
    return pl.pallas_call(
        lookup_kernel, out_shape=pltpu.VMEM((slots, LANES), jnp.bfloat16), name="lookup"
    )(triplets, codes.reshape(-1, WIDE))


def triplet_stage(data, slot_rows, cotangent):
    blocks = data.shape[0]
    slots = slot_rows.shape[0]
    cells = blocks * LANES
    keep = 4 * slots * cells <= KEEP_BYTES
    kept = cells if keep else math.gcd(CELL_STEP, cells)
    return pl.pallas_call(
        functools.partial(main_kernel, keep, 1.0 / math.sqrt(cells)),
        out_shape=(
            jax.ShapeDtypeStruct(cotangent.shape, jnp.float32),
            pltpu.VMEM((blocks, 8, LANES), jnp.float32),
        ),
        scratch_shapes=[
            pltpu.VMEM((DEPTH, cells), jnp.bfloat16),
            pltpu.VMEM((8, cells), jnp.bfloat16),
            pltpu.VMEM((16, slots), jnp.float32),
            pltpu.VMEM((slots, kept), jnp.bfloat16),
            pltpu.VMEM((slots, kept), jnp.bfloat16),
        ],
        in_specs=[pl.BlockSpec(memory_space=pltpu.VMEM)] * 3,
        name="triplet_stage",
    )(data, slot_rows, cotangent)


def reduce_cells(blocks):
    return lax.all_to_all(blocks, "cell", 0, 0).sum(0)


def pack_kernel(place_ref, weight_ref, out_ref):
    place = place_ref[...]
    place = place - jnp.round(place)
    high = place.astype(jnp.bfloat16).astype(jnp.float32)
    rest = place - high
    middle = rest.astype(jnp.bfloat16).astype(jnp.float32)
    none = jnp.zeros((DEPTH - 9, place.shape[1]), jnp.float32)
    rows = [high, middle, rest - middle, none, weight_ref[...].astype(jnp.float32)]
    block = jnp.concatenate(rows, axis=0).astype(jnp.bfloat16)
    for i in range(out_ref.shape[0]):
        out_ref[i] = block


def pack(positions, weights, devices):
    return pl.pallas_call(
        pack_kernel, out_shape=jax.ShapeDtypeStruct((devices, ROWS, positions.shape[1]), jnp.bfloat16), name="pack"
    )(positions, weights)


def on_device(momenta, positions, weights, triplets, cotangent):
    devices = lax.axis_size("cell")
    data = lax.all_to_all(pack(positions, weights, devices), "cell", 0, 0)
    data = pltpu.with_memory_space_constraint(data, pltpu.VMEM)
    slot_rows = pltpu.with_memory_space_constraint(lookup(triplets, momenta), pltpu.VMEM)
    correlation, partial = triplet_stage(data, slot_rows, cotangent)
    return correlation, reduce_cells(partial)


def solution(mesh):
    split = P(None, ("grp", "cell"))
    return jax.shard_map(
        on_device,
        mesh=mesh,
        in_specs=(P(), split, split, split, split),
        out_specs=(split, split),
        check_vma=False,
    )
```
